32 devices in a mesh: ent: 8 (over z, y), rep: 4 (over x, core).
Axes of the slice: x: 2, y: 2, z: 4, core: 2. Of those that a mesh axis runs over, the one named last changes fastest.
Arguments:
- facts: bfloat16 [65536, 512], P(('ent', 'rep')), may hold values from -6 to 6
- fact_owner: int32 [65536, 1], P(('ent', 'rep')), may hold values from 0 to 7; in each aligned block of 2048 rows (0 to 2047, 2048 to 4095, ...) at most 512 rows name the same one
- fact_slot: int32 [65536], P(('ent', 'rep')), may hold values from 0 to 127
- entity_feats: bfloat16 [1024, 512], P('ent'), may hold values from -6 to 6
- out_cotangent: bfloat16 [1024, 512], P('ent'), may hold values from -6 to 6
- w_msg: bfloat16 [512, 512], replicated, may hold values from -0.25 to 0.25
- w_upd: bfloat16 [512, 512], replicated, may hold values from -0.25 to 0.25
Outputs:
- ent_out: bfloat16 [1024, 512], P('ent')
- fact_grad: bfloat16 [65536, 512], P(('ent', 'rep'))
- msg_weight_grad: float32 [512, 512], P(('ent', 'rep'))
- upd_weight_grad_t: float32 [512, 512], P(('ent', 'rep'))
The draws below stay inside these ranges and needn't reach their ends.
Inputs may be any that keep to these rules, and one draw needn't show every extreme that they name: `fact_owner`: among the rows of one device, at most 512 name the same owner.
All inputs are finite; a program needn't handle non-finite values.
Results may differ from the reference program's by a relative error of at most 0.0065.
Values may be sent and summed in bfloat16 or wider, within the bound.
A program may use at most 64 MiB of HBM per device.

```python
import math
import jax
import jax.numpy as jnp
import numpy as np
from jax import lax

D = 512
F_DEV = 2048
ENT_DEV = 128
CAP = 512
FACTS = 65536
ENTS = 1024
N_ENT = 8


def with_ends(entries, key, smallest, high):
    spot = [jax.random.randint(jax.random.fold_in(key, axis), (), 0, length) for axis, length in enumerate(entries.shape)]
    longest = entries.shape.index(max(entries.shape))
    neighbour = spot[:longest] + [(spot[longest] + 1) % entries.shape[longest]] + spot[longest + 1:]
    return entries.at[tuple(spot)].set(smallest).at[tuple(neighbour)].set(high)


def spiked(entries, own_key, source, target, parts, factor):
    owner, partner = [(jnp.arange(entries.shape[axis_at]) // (entries.shape[axis_at] // parts)).reshape([-1 if axis == axis_at else 1 for axis in range(entries.ndim)]) for axis_at in (source, target)]
    chosen = jax.random.permutation(own_key, parts)[partner]
    strong = (owner == chosen) | (owner == (partner + parts // 2) % parts)
    return jnp.where(strong, factor * entries, entries)


def level_of(stream_key, extent, cuts, smallest, largest):
    def one(position, shards_of):
        steps = jax.random.uniform(jax.random.fold_in(jax.random.fold_in(stream_key, 6), position), (shards_of,), jnp.float32, smallest / len(cuts), largest / len(cuts))
        return jnp.repeat(jnp.exp(steps), extent[position] // shards_of).reshape((-1,) + (1,) * (len(extent) - position - 1))

    loudness = one(*cuts[0])
    for cut in cuts[1:]:
        loudness = loudness * one(*cut)
    return loudness


def rank_bounds(amount, slope):
    portions = [(1 << 20) // math.isqrt(standing ** slope) + 1 for standing in range(1, amount + 1)]
    deviation = 1 + sum(portions) // (1 << 30)
    return np.cumsum(np.array([max(1, weight // deviation) for weight in portions]))


def skewed_ids(stream_key, dims, number_of, slope):
    listing = rank_bounds(number_of, slope)
    pick = jax.random.randint(jax.random.fold_in(stream_key, 1), dims, 0, int(listing[number_of - 1]))
    grade = jnp.searchsorted(jnp.asarray(listing, jnp.int32), pick, side="right")
    return jax.random.permutation(jax.random.fold_in(stream_key, 2), number_of)[grade].astype(jnp.int32)


def deal_out(rng, own, number, rows, amount, top, most, skew):
    order = jax.random.permutation(rng, amount)
    crowded, ordinary = portions_of(amount, rows * top, most, skew, True), portions_of(amount, rows * top, most, skew, False)
    places = jnp.arange(amount)

    def named(sizes, turn):
        used = int((sizes > 0).sum())
        fixed = max(1, used // 4)
        moved = fixed + (places - fixed + turn * (used - fixed)) % max(1, amount - fixed)
        return jnp.zeros((amount,), jnp.int32).at[order[jnp.where(places < fixed, places, moved)]].set(jnp.asarray(sizes, jnp.int32))

    sizes = jnp.where(number % 4 == 0, named(crowded, number // 4), named(ordinary, number - number // 4 - 1))
    mixed = jax.random.permutation(jax.random.fold_in(own, 3), amount)
    source_of, sink = mixed[0:amount // 2 * 2:2], mixed[1:amount // 2 * 2:2]
    slack = jnp.minimum(sizes[source_of] - 1, most - sizes[sink]) // 2
    slack = jnp.where((source_of == order[0]) | (sink == order[0]) | (sizes[sink] == 0), 0, jnp.maximum(slack, 0))
    moved = jax.random.randint(jax.random.fold_in(own, 4), (amount // 2,), 0, 1 << 20) % (slack + 1)
    sizes = sizes.at[source_of].add(-moved).at[sink].add(moved)
    items = jnp.searchsorted(jnp.cumsum(sizes), jnp.arange(rows * top), side="right").astype(jnp.int32)
    grid = items.reshape(top, rows).T
    grid = grid[jax.random.permutation(jax.random.fold_in(own, 1), rows)]
    turn = jax.random.randint(jax.random.fold_in(own, 2), (rows, 1), 0, top)
    return jnp.take_along_axis(grid, (jnp.arange(top)[None, :] + turn) % top, axis=1)


def portions_of(number_of, total, most, lean, full):
    loads = [(1 << 20) // math.isqrt(rank ** lean) + 1 for rank in range(1, number_of + 1)]
    largest = most if full else min(most, max(-(-total // number_of), total * loads[0] // sum(loads)))
    least = 1 if total - largest >= number_of - 1 else 0
    counts, surplus = [largest] + [least] * (number_of - 1), total - largest - least * (number_of - 1)
    while surplus > 0:
        free = [i for i in range(1, number_of) if counts[i] < largest] or [i for i in range(1, number_of) if counts[i] < most]
        whole, left = sum([loads[i] for i in free]), surplus
        for i in free:
            extra = min(most - counts[i], max(1, left * loads[i] // whole), surplus)
            counts[i] = counts[i] + extra
            surplus = surplus - extra
    return np.array(counts)


def bell_draw(stream_key, shape, spread, bound, split=(), dtype=jnp.bfloat16):
    loudness = level_of(stream_key, shape, split, -0.22, 0.18) if split else 1.0
    values = jax.random.normal(stream_key, shape, jnp.float32) * spread * loudness
    return jnp.minimum(jnp.maximum(values, -bound), bound).astype(dtype)


def heavy_noise(key, extent, deviation, most, cuts, heavy, kind=jnp.bfloat16):
    array = deviation * jax.random.normal(key, extent, jnp.float32)
    if cuts:
        array = array * level_of(key, extent, cuts, -0.22, 0.18)
    return jnp.clip(spiked(array, jax.random.fold_in(key, 3), *heavy), -most, most).astype(kind)


def setup_inputs(seed: int = 0) -> dict:
    key_of = jax.random.split(jax.random.key(seed), 8)
    facts = heavy_noise(key_of[0], (FACTS, D), 1.0, 6.0, ((0, 32),), (0, 1, 32, 2.75))
    fact_owner_keys = jax.random.split(jax.random.fold_in(key_of[1], 1), FACTS // F_DEV)
    fact_owner_turns = jax.random.permutation(jax.random.fold_in(key_of[1], 3), FACTS // F_DEV)
    fact_owner = jax.vmap(lambda own, number: deal_out(jax.random.fold_in(key_of[1], 2), own, number, F_DEV, N_ENT, 1, CAP, 2))(fact_owner_keys, fact_owner_turns).reshape((FACTS, 1))
    fact_slot = with_ends(skewed_ids(key_of[2], (FACTS,), ENT_DEV, 2), jax.random.fold_in(key_of[2], 3), 0, ENT_DEV - 1).astype(jnp.int32)
    entity_feats = bell_draw(key_of[3], (ENTS, D), 1.0, 6.0, ((0, 8),))
    out_cotangent = heavy_noise(key_of[4], (ENTS, D), 1.0, 6.0, ((0, 8),), (0, 1, 8, 2.0))
    w_msg = bell_draw(key_of[5], (D, D), D ** -0.5, 0.25)
    w_upd = bell_draw(key_of[6], (D, D), D ** -0.5, 0.25)
    return {"facts": facts, "fact_owner": fact_owner, "fact_slot": fact_slot, "entity_feats": entity_feats, "out_cotangent": out_cotangent, "w_msg": w_msg, "w_upd": w_upd}


def silu_grad(value):
    sig = jax.nn.sigmoid(value)
    return sig * (1.0 + value * (1.0 - sig))

def reference(facts, fact_owner, fact_slot, entity_feats, out_cotangent, w_msg, w_upd):
    key = (fact_owner[:, 0] * ENT_DEV + fact_slot).astype(jnp.int32)
    pre = jnp.dot(facts, w_msg, preferred_element_type=jnp.float32)
    message = jax.nn.silu(pre).astype(jnp.bfloat16)
    total = ENT_DEV * N_ENT
    agg = jax.ops.segment_sum(message.astype(jnp.float32), key, num_segments=total)
    count = jax.ops.segment_sum(jnp.ones(key.shape, jnp.float32), key, num_segments=total)
    denom = jnp.maximum(count, 1.0)[:, None]
    mean = (agg / denom).astype(jnp.bfloat16)
    zval = jnp.dot(mean, w_upd, preferred_element_type=jnp.float32)
    ent_out = (entity_feats.astype(jnp.float32) + jax.nn.silu(zval)).astype(jnp.bfloat16)
    grad_z = (out_cotangent.astype(jnp.float32) * silu_grad(zval)).astype(jnp.bfloat16)
    upd_t = lax.dot_general(grad_z, mean, (((0,), (0,)), ((), ())), preferred_element_type=jnp.float32)
    d_mean = lax.dot_general(grad_z, w_upd, (((1,), (1,)), ((), ())), preferred_element_type=jnp.float32)
    d_agg = (d_mean / denom).astype(jnp.bfloat16)
    d_msg = jnp.take(d_agg, key, axis=0)
    d_pre = (d_msg.astype(jnp.float32) * silu_grad(pre)).astype(jnp.bfloat16)
    msg_grad = lax.dot_general(facts, d_pre, (((0,), (0,)), ((), ())), preferred_element_type=jnp.float32)
    fact_grad = lax.dot_general(d_pre, w_msg, (((1,), (1,)), ((), ())), preferred_element_type=jnp.float32).astype(jnp.bfloat16)
    return (ent_out, fact_grad, msg_grad, upd_t)
```

```python
import jax
import jax.numpy as jnp
from jax import lax
from jax.sharding import PartitionSpec as P


def silu_grad(value):
    sig = jax.nn.sigmoid(value)
    return sig * (1.0 + value * (1.0 - sig))


def per_device(facts, fact_owner, fact_slot, entity_feats, out_cotangent, w_msg, w_upd):
    n_owners = lax.axis_size("ent")
    n_copies = lax.axis_size("rep")
    width = facts.shape[1]
    ent_rows = entity_feats.shape[0]
    ents = ent_rows * n_owners
    share = ent_rows // n_copies
    key = fact_owner[:, 0] * ent_rows + fact_slot
    onehot = (jnp.arange(ents, dtype=jnp.int32)[:, None] == key[None, :]).astype(jnp.bfloat16)
    pre = jnp.dot(facts, w_msg, preferred_element_type=jnp.float32)
    message = jax.nn.silu(pre).astype(jnp.bfloat16)
    part_agg = jnp.dot(onehot, message, preferred_element_type=jnp.float32)
    part_count = jnp.sum(onehot, axis=1, dtype=jnp.float32)
    part = jnp.concatenate([part_agg, jnp.broadcast_to(part_count[:, None], (ents, 128))], axis=1)
    both = lax.psum_scatter(part, ("ent", "rep"), scatter_dimension=0, tiled=True)
    agg = both[:, :width]
    denom = jnp.maximum(both[:, width:width + 1], 1.0)
    begin = lax.axis_index("rep") * share
    feats = lax.dynamic_slice_in_dim(entity_feats, begin, share, 0)
    cot = lax.dynamic_slice_in_dim(out_cotangent, begin, share, 0)
    mean = (agg / denom).astype(jnp.bfloat16)
    zval = jnp.dot(mean, w_upd, preferred_element_type=jnp.float32)
    ent_part = (feats.astype(jnp.float32) + jax.nn.silu(zval)).astype(jnp.bfloat16)
    grad_z = (cot.astype(jnp.float32) * silu_grad(zval)).astype(jnp.bfloat16)
    d_mean = lax.dot_general(
        grad_z, w_upd, (((1,), (1,)), ((), ())), preferred_element_type=jnp.float32
    )
    d_agg = (d_mean / denom).astype(jnp.bfloat16)
    d_all = lax.all_gather(d_agg, ("ent", "rep"), axis=0, tiled=True)
    ent_out = lax.all_gather(ent_part, "rep", axis=0, tiled=True)
    d_msg = lax.dot_general(
        onehot, d_all, (((0,), (0,)), ((), ())), preferred_element_type=jnp.float32
    )
    d_pre = (d_msg * silu_grad(pre)).astype(jnp.bfloat16)
    fact_grad = lax.dot_general(
        d_pre, w_msg, (((1,), (1,)), ((), ())), preferred_element_type=jnp.float32
    ).astype(jnp.bfloat16)
    left = lax.dot_general(
        facts, d_pre, (((0,), (0,)), ((), ())), preferred_element_type=jnp.float32
    )
    right = lax.dot_general(
        grad_z, mean, (((0,), (0,)), ((), ())), preferred_element_type=jnp.float32
    )
    grads = lax.psum_scatter(
        jnp.concatenate([left, right], axis=1), ("ent", "rep"), scatter_dimension=0, tiled=True
    )
    return (ent_out, fact_grad, grads[:, :width], grads[:, width:])


def solution(mesh):
    placed = (
        P(("ent", "rep"), None),
        P(("ent", "rep"), None),
        P(("ent", "rep")),
        P("ent", None),
        P("ent", None),
        P(),
        P(),
    )
    return jax.shard_map(
        per_device,
        mesh=mesh,
        in_specs=placed,
        out_specs=(
            P("ent", None),
            P(("ent", "rep"), None),
            P(("ent", "rep"), None),
            P(("ent", "rep"), None),
        ),
        check_vma=False,
    )
```

```python
import functools

import jax
import jax.numpy as jnp
from jax import lax
from jax.experimental import pallas as pl
from jax.experimental.pallas import tpu as pltpu
from jax.sharding import PartitionSpec as P

E_HI, E_LO, R_HI, R_LO = range(4)
ORDER_A = (R_LO, R_HI, E_LO, E_HI)
ORDER_B = (R_LO, E_LO, R_HI, E_HI)
MESH = pl.DeviceIdType.MESH
VMEM_LIMIT = 56 << 20


def silu_grad(value):
    sig = jax.nn.sigmoid(value)
    return sig * (1.0 + value * (1.0 - sig))


def position():
    ent, rep = lax.axis_index("ent"), lax.axis_index("rep")
    return (ent // 2, lax.rem(ent, 2), rep // 2, lax.rem(rep, 2))


def device_at(here, dim, coord):
    if dim == E_HI:
        return {"ent": coord * 2 + here[E_LO]}
    if dim == E_LO:
        return {"ent": here[E_HI] * 2 + coord}
    if dim == R_HI:
        return {"rep": coord * 2 + here[R_LO]}
    return {"rep": here[R_HI] * 2 + coord}


def enter(grid, here):
    barrier = pltpu.get_barrier_semaphore()
    rep = here[R_HI] * 2 + here[R_LO]
    n_rep = grid[R_HI] * grid[R_LO]
    total = 0
    for step in range(1, n_rep):
        pl.semaphore_signal(
            barrier, inc=1, device_id={"rep": lax.rem(rep + step, n_rep)}, device_id_type=MESH
        )
        total += 1
    for dim in (E_HI, E_LO):
        for step in range(1, grid[dim]):
            target = device_at(here, dim, lax.rem(here[dim] + step, grid[dim]))
            pl.semaphore_signal(barrier, inc=1, device_id=target, device_id_type=MESH)
            total += 1
    pl.semaphore_wait(barrier, total)


def sum_scratch(grid, order, tail, dtype):
    left, shapes = [0, 1, 2, 3], []
    for dim in order:
        left.remove(dim)
        kept = tuple(grid[d] for d in left) + tail
        final = not left
        shapes += [
            pltpu.VMEM((grid[dim] - 1,) + kept, dtype),
            pltpu.VMEM(kept, jnp.float32 if final else dtype),
            pltpu.SemaphoreType.DMA((grid[dim] - 1,)),
            pltpu.SemaphoreType.DMA((grid[dim] - 1,)),
        ]
    return shapes


class Scatter:
    def __init__(self, grid, here, order, source, scratch):
        self.grid, self.here, self.order, self.current = grid, here, order, source
        self.scratch, self.left, self.stage = scratch, [0, 1, 2, 3], 0

    def start(self):
        dim = self.order[self.stage]
        size, mine = self.grid[dim], self.here[dim]
        arrived, _, send, recv = self.scratch[4 * self.stage:4 * self.stage + 4]
        lead = (slice(None),) * self.left.index(dim)
        self.copies = []
        for step in range(1, size):
            coord = lax.rem(mine + step, size)
            copy = pltpu.make_async_remote_copy(
                src_ref=self.current.at[lead + (coord,)],
                dst_ref=arrived.at[step - 1],
                send_sem=send.at[step - 1],
                recv_sem=recv.at[step - 1],
                device_id=device_at(self.here, dim, coord),
                device_id_type=MESH,
            )
            copy.start()
            self.copies.append(copy)

    def finish(self):
        dim = self.order[self.stage]
        arrived, total, _, _ = self.scratch[4 * self.stage:4 * self.stage + 4]
        lead = (slice(None),) * self.left.index(dim)
        value = self.current[lead + (self.here[dim],)].astype(jnp.float32)
        for index, copy in enumerate(self.copies):
            copy.wait()
            value = value + arrived[index].astype(jnp.float32)
        total[...] = value.astype(total.dtype)
        self.current = total
        self.left.remove(dim)
        self.stage += 1


class Gather:
    def __init__(self, grid, here, order, columns, ref, sems):
        self.grid, self.here, self.order = grid, here, order
        self.columns, self.ref, self.sems = columns, ref, sems
        self.done, self.stage = [], 0

    def start(self):
        dim = self.order[self.stage]
        size, mine = self.grid[dim], self.here[dim]
        send, recv = self.sems[2 * self.stage:2 * self.stage + 2]
        index = tuple(slice(None) if d in self.done else self.here[d] for d in range(4))
        block = self.ref.at[index + (slice(None), self.columns)]
        self.copies = []
        for step in range(1, size):
            coord = lax.rem(mine + step, size)
            copy = pltpu.make_async_remote_copy(
                src_ref=block,
                dst_ref=block,
                send_sem=send.at[step - 1],
                recv_sem=recv.at[step - 1],
                device_id=device_at(self.here, dim, coord),
                device_id_type=MESH,
            )
            copy.start()
            self.copies.append(copy)

    def finish(self):
        for copy in self.copies:
            copy.wait()
        self.done.append(self.order[self.stage])
        self.stage += 1


def gather_scratch(grid, order):
    return [pltpu.SemaphoreType.DMA((grid[d] - 1,)) for d in order for _ in range(2)]


def entity_kernel(grid, part_ref, count_ref, feats_ref, cot_ref, w_ref,
                  all_ref, ent_ref, mean_ref, gz_ref, *scratch):
    here = position()
    rep = lax.axis_index("rep")
    n_rep = grid[R_HI] * grid[R_LO]
    half = part_ref.shape[-1] // 2
    share = part_ref.shape[-2]
    enter(grid, here)
    every = (slice(None),) * 5
    sums = [
        Scatter(grid, here, ORDER_A, count_ref, scratch[0:16]),
        Scatter(grid, here, ORDER_A, part_ref.at[every + (slice(0, half),)], scratch[16:32]),
        Scatter(grid, here, ORDER_B, part_ref.at[every + (slice(half, 2 * half),)], scratch[32:48]),
    ]
    for item in sums:
        item.start()
    for stage in range(4):
        for item in sums:
            item.finish()
            if stage < 3:
                item.start()
    lane = lax.broadcasted_iota(jnp.int32, (share, 128), 1)
    row = lax.broadcasted_iota(jnp.int32, (share, 128), 0)
    counts = jnp.broadcast_to(sums[0].current[0:1, :], (share, 128))
    count = jnp.sum(jnp.where(lane == row, counts, 0.0), axis=1, keepdims=True)
    denom = jnp.maximum(count, 1.0)
    agg = jnp.concatenate([sums[1].current[...], sums[2].current[...]], axis=1)
    mean = (agg / denom).astype(jnp.bfloat16)
    zval = jnp.dot(mean, w_ref[...], preferred_element_type=jnp.float32)
    grad_z = (cot_ref[rep].astype(jnp.float32) * silu_grad(zval)).astype(jnp.bfloat16)
    d_mean = lax.dot_general(
        grad_z, w_ref[...], (((1,), (1,)), ((), ())), preferred_element_type=jnp.float32
    )
    all_ref[here] = (d_mean / denom).astype(jnp.bfloat16)
    spreads = [
        Gather(grid, here, ORDER_A[::-1], slice(0, half), all_ref, scratch[48:56]),
        Gather(grid, here, ORDER_B[::-1], slice(half, 2 * half), all_ref, scratch[56:64]),
    ]
    for item in spreads:
        item.start()
    mean_ref[...] = mean
    gz_ref[...] = grad_z
    ent_ref[rep] = (feats_ref[rep].astype(jnp.float32) + zval * jax.nn.sigmoid(zval)).astype(
        jnp.bfloat16
    )
    ent_copies = []
    for step in range(1, n_rep):
        copy = pltpu.make_async_remote_copy(
            src_ref=ent_ref.at[rep],
            dst_ref=ent_ref.at[rep],
            send_sem=scratch[64].at[step - 1],
            recv_sem=scratch[65].at[step - 1],
            device_id={"rep": lax.rem(rep + step, n_rep)},
            device_id_type=MESH,
        )
        copy.start()
        ent_copies.append(copy)
    for stage in range(4):
        for item in spreads:
            item.finish()
            if stage < 3:
                item.start()
    for copy in ent_copies:
        copy.wait()


def grads_kernel(grid, left_ref, right_ref, d_pre_ref, w_ref, msg_ref, upd_ref, fact_ref, *scratch):
    here = position()
    enter(grid, here)
    sums = [
        Scatter(grid, here, ORDER_A, left_ref, scratch[0:16]),
        Scatter(grid, here, ORDER_B, right_ref, scratch[16:32]),
    ]
    for item in sums:
        item.start()
    rows = d_pre_ref.shape[0] // 4
    for stage in range(4):
        part = pl.ds(stage * rows, rows)
        fact_ref[part, :] = lax.dot_general(
            d_pre_ref[part, :], w_ref[...], (((1,), (1,)), ((), ())),
            preferred_element_type=jnp.float32,
        ).astype(jnp.bfloat16)
        for item in sums:
            item.finish()
            if stage < 3:
                item.start()
    msg_ref[...] = sums[0].current[...]
    upd_ref[...] = sums[1].current[...]


def in_vmem(number):
    return [pl.BlockSpec(memory_space=pltpu.VMEM)] * number


def per_device(facts, fact_owner, fact_slot, entity_feats, out_cotangent, w_msg, w_upd):
    n_owners = lax.axis_size("ent")
    n_copies = lax.axis_size("rep")
    grid = (n_owners // 2, 2, n_copies // 2, 2)
    fact_rows, width = facts.shape
    ent_rows = entity_feats.shape[0]
    ents = ent_rows * n_owners
    share = ent_rows // n_copies
    bf16, f32 = jnp.bfloat16, jnp.float32
    key = fact_owner[:, 0] * ent_rows + fact_slot
    onehot = (jnp.arange(ents, dtype=jnp.int32)[:, None] == key[None, :]).astype(bf16)
    pre = jnp.dot(facts, w_msg, preferred_element_type=f32)
    message = jax.nn.silu(pre).astype(bf16)
    part = jnp.dot(onehot, message, preferred_element_type=f32).astype(bf16)
    count = jnp.sum(onehot, axis=1, dtype=f32).reshape(grid + (1, share))
    count = jnp.broadcast_to(jnp.pad(count, ((0, 0),) * 5 + ((0, 128 - share),)), grid + (8, 128))
    rep_sem = pltpu.SemaphoreType.DMA((n_copies - 1,))
    d_all, ent_out, mean, grad_z = pl.pallas_call(
        functools.partial(entity_kernel, grid),
        out_shape=(
            jax.ShapeDtypeStruct(grid + (share, width), bf16),
            jax.ShapeDtypeStruct((n_copies, share, width), bf16),
            jax.ShapeDtypeStruct((share, width), bf16),
            jax.ShapeDtypeStruct((share, width), bf16),
        ),
        in_specs=in_vmem(5),
        out_specs=in_vmem(4),
        scratch_shapes=(
            sum_scratch(grid, ORDER_A, (8, 128), f32)
            + sum_scratch(grid, ORDER_A, (share, width // 2), bf16)
            + sum_scratch(grid, ORDER_B, (share, width // 2), bf16)
            + gather_scratch(grid, ORDER_A[::-1])
            + gather_scratch(grid, ORDER_B[::-1])
            + [rep_sem, rep_sem]
        ),
        compiler_params=pltpu.CompilerParams(
            collective_id=0, has_side_effects=True, vmem_limit_bytes=VMEM_LIMIT
        ),
    )(
        part.reshape(grid + (share, width)),
        count,
        entity_feats.reshape(n_copies, share, width),
        out_cotangent.reshape(n_copies, share, width),
        w_upd,
    )
    d_msg = lax.dot_general(
        onehot, d_all.reshape(ents, width), (((0,), (0,)), ((), ())), preferred_element_type=f32
    )
    d_pre = (d_msg * silu_grad(pre)).astype(bf16)
    left = lax.dot_general(
        facts, d_pre, (((0,), (0,)), ((), ())), preferred_element_type=f32
    ).astype(bf16)
    right = lax.dot_general(
        grad_z, mean, (((0,), (0,)), ((), ())), preferred_element_type=f32
    ).astype(bf16)
    rows = width // (n_owners * n_copies)
    msg_grad, upd_grad, fact_grad = pl.pallas_call(
        functools.partial(grads_kernel, grid),
        out_shape=(
            jax.ShapeDtypeStruct((rows, width), f32),
            jax.ShapeDtypeStruct((rows, width), f32),
            jax.ShapeDtypeStruct((fact_rows, width), bf16),
        ),
        in_specs=in_vmem(4),
        out_specs=in_vmem(3),
        scratch_shapes=(
            sum_scratch(grid, ORDER_A, (rows, width), bf16)
            + sum_scratch(grid, ORDER_B, (rows, width), bf16)
        ),
        compiler_params=pltpu.CompilerParams(
            collective_id=1, has_side_effects=True, vmem_limit_bytes=VMEM_LIMIT
        ),
    )(left.reshape(grid + (rows, width)), right.reshape(grid + (rows, width)), d_pre, w_msg)
    return (ent_out.reshape(ent_rows, width), fact_grad, msg_grad, upd_grad)


def solution(mesh):
    placed = (
        P(("ent", "rep"), None),
        P(("ent", "rep"), None),
        P(("ent", "rep")),
        P("ent", None),
        P("ent", None),
        P(),
        P(),
    )
    return jax.shard_map(
        per_device,
        mesh=mesh,
        in_specs=placed,
        out_specs=(
            P("ent", None),
            P(("ent", "rep"), None),
            P(("ent", "rep"), None),
            P(("ent", "rep"), None),
        ),
        check_vma=False,
    )
```

```python
import functools

import jax
import jax.numpy as jnp
from jax import lax
from jax.experimental import pallas as pl
from jax.experimental.pallas import tpu as pltpu
from jax.sharding import PartitionSpec as P

E_HI, E_LO, R_HI, R_LO = range(4)
ORDER_A = (R_LO, R_HI, E_LO, E_HI)
ORDER_B = (R_LO, E_LO, R_HI, E_HI)
MESH = pl.DeviceIdType.MESH
VMEM_LIMIT = 56 << 20


def silu_grad(value):
    sig = jax.nn.sigmoid(value)
    return sig * (1.0 + value * (1.0 - sig))


def position():
    ent, rep = lax.axis_index("ent"), lax.axis_index("rep")
    return (ent // 2, lax.rem(ent, 2), rep // 2, lax.rem(rep, 2))


def device_at(here, dim, coord):
    if dim == E_HI:
        return {"ent": coord * 2 + here[E_LO]}
    if dim == E_LO:
        return {"ent": here[E_HI] * 2 + coord}
    if dim == R_HI:
        return {"rep": coord * 2 + here[R_LO]}
    return {"rep": here[R_HI] * 2 + coord}


def greet(grid, here):
    barrier = pltpu.get_barrier_semaphore()
    rep = here[R_HI] * 2 + here[R_LO]
    n_rep = grid[R_HI] * grid[R_LO]
    total = 0
    for step in range(1, n_rep):
        pl.semaphore_signal(
            barrier, inc=1, device_id={"rep": lax.rem(rep + step, n_rep)}, device_id_type=MESH
        )
        total += 1
    for dim in (E_HI, E_LO):
        for step in range(1, grid[dim]):
            target = device_at(here, dim, lax.rem(here[dim] + step, grid[dim]))
            pl.semaphore_signal(barrier, inc=1, device_id=target, device_id_type=MESH)
            total += 1
    return total


def sum_scratch(grid, order, tail, dtype):
    left, shapes = [0, 1, 2, 3], []
    for dim in order:
        left.remove(dim)
        kept = tuple(grid[d] for d in left) + tail
        shapes += [
            pltpu.VMEM((grid[dim] - 1,) + kept, dtype),
            pltpu.VMEM(kept, jnp.float32),
            pltpu.VMEM(kept if left else (16, 128), dtype),
            pltpu.SemaphoreType.DMA((grid[dim] - 1,)),
            pltpu.SemaphoreType.DMA((grid[dim] - 1,)),
        ]
    return shapes


class Scatter:
    def __init__(self, grid, here, order, own, sent, scratch):
        self.grid, self.here, self.order, self.own, self.sent = grid, here, order, own, sent
        self.scratch, self.left, self.stage = scratch, [0, 1, 2, 3], 0

    def start(self):
        dim = self.order[self.stage]
        size, mine = self.grid[dim], self.here[dim]
        arrived, _, _, send, recv = self.scratch[5 * self.stage:5 * self.stage + 5]
        lead = (slice(None),) * self.left.index(dim)
        self.copies = []
        for step in range(1, size):
            coord = lax.rem(mine + step, size)
            copy = pltpu.make_async_remote_copy(
                src_ref=self.sent.at[lead + (coord,)],
                dst_ref=arrived.at[step - 1],
                send_sem=send.at[step - 1],
                recv_sem=recv.at[step - 1],
                device_id=device_at(self.here, dim, coord),
                device_id_type=MESH,
            )
            copy.start()
            self.copies.append(copy)

    def finish(self):
        dim = self.order[self.stage]
        arrived, total, rounded, _, _ = self.scratch[5 * self.stage:5 * self.stage + 5]
        lead = (slice(None),) * self.left.index(dim)
        value = self.own[lead + (self.here[dim],)]
        for index, copy in enumerate(self.copies):
            copy.wait()
            value = value + arrived[index].astype(jnp.float32)
        total[...] = value
        self.own = self.sent = total
        self.left.remove(dim)
        self.stage += 1
        if self.left and rounded.dtype != jnp.float32:
            rounded[...] = value.astype(rounded.dtype)
            self.sent = rounded

    def advance(self):
        self.finish()
        if self.stage < 4:
            self.start()


class Gather:
    def __init__(self, grid, here, order, columns, ref, sems):
        self.grid, self.here, self.order = grid, here, order
        self.columns, self.ref, self.sems = columns, ref, sems
        self.done, self.stage = [], 0

    def start(self):
        dim = self.order[self.stage]
        size, mine = self.grid[dim], self.here[dim]
        send, recv = self.sems[2 * self.stage:2 * self.stage + 2]
        index = tuple(slice(None) if d in self.done else self.here[d] for d in range(4))
        block = self.ref.at[index + (slice(None), self.columns)]
        self.copies = []
        for step in range(1, size):
            coord = lax.rem(mine + step, size)
            copy = pltpu.make_async_remote_copy(
                src_ref=block,
                dst_ref=block,
                send_sem=send.at[step - 1],
                recv_sem=recv.at[step - 1],
                device_id=device_at(self.here, dim, coord),
                device_id_type=MESH,
            )
            copy.start()
            self.copies.append(copy)

    def advance(self):
        for copy in self.copies:
            copy.wait()
        self.done.append(self.order[self.stage])
        self.stage += 1
        if self.stage < 4:
            self.start()


def gather_scratch(grid, order):
    return [pltpu.SemaphoreType.DMA((grid[d] - 1,)) for d in order for _ in range(2)]


def layer_kernel(grid, facts_ref, key_ref, feats_ref, cot_ref, w_ref, w_upd_ref,
                 d_pre_ref, ent_ref, grads_ref, *scratch):
    bf16, f32 = jnp.bfloat16, jnp.float32
    here = position()
    rep = lax.axis_index("rep")
    n_rep = grid[R_HI] * grid[R_LO]
    greeted = greet(grid, here)
    scratch = list(scratch)

    def take(number):
        taken, scratch[:number] = scratch[:number], []
        return taken

    gate_ref, part_ref, part_sent, hot_ref, facts_t, all_ref, count_ref = take(7)
    side_ref, side_sent, left_ref, left_sent = take(4)
    message_ref = d_pre_ref
    fact_rows, width = facts_ref.shape
    half = width // 2
    halves = [slice(0, half), slice(half, width)]
    share = part_ref.shape[-2]
    ent_rows = share * n_rep
    block = fact_rows // 4
    pair = 2 * ent_rows
    kept = hot_ref.shape[0] > pair
    every = (slice(None),) * 5
    counts = Scatter(grid, here, ORDER_A, count_ref, count_ref, take(20))
    sums = [
        Scatter(grid, here, order, part_ref.at[every + (cols,)], part_sent.at[every + (cols,)],
                take(20))
        for order, cols in zip((ORDER_A, ORDER_B), halves)
    ]
    spreads = [
        Gather(grid, here, order[::-1], cols, all_ref, take(8))
        for order, cols in zip((ORDER_A, ORDER_B), halves)
    ]
    sides = Scatter(grid, here, ORDER_A, side_ref, side_sent, take(20))
    lefts = [
        Scatter(grid, here, order, left_ref.at[every + (cols,)], left_sent.at[every + (cols,)],
                take(20))
        for order, cols in zip((ORDER_A, ORDER_B), halves)
    ]
    ent_send, ent_recv = take(2)

    for number, cols in enumerate(halves):

        def project(step, carry, cols=cols):
            rows = pl.ds(pl.multiple_of(step * block, block), block)
            pre = jnp.dot(facts_ref[rows, :], w_ref[:, cols], preferred_element_type=f32)
            sig = jax.nn.sigmoid(pre)
            gate_ref[rows, cols] = sig * (1.0 + pre * (1.0 - sig))
            message_ref[rows, cols] = (pre * sig).astype(bf16)
            return carry

        lax.fori_loop(0, 4, project, 0)

        def gather_sums(step, carry, number=number, cols=cols):
            rows = pl.ds(pl.multiple_of(step * pair, pair), pair) if kept else pl.ds(0, pair)
            if number == 0 or not kept:
                ids = lax.broadcasted_iota(jnp.int32, (pair, fact_rows), 0) + step * pair
                hit = (ids == key_ref[...]).astype(f32)
                hot_ref[rows, :] = hit.astype(bf16)
                if number == 0:
                    total = jnp.sum(hit, axis=1, keepdims=True)
                    for low in range(2):
                        column = jnp.broadcast_to(
                            total[low * ent_rows:(low + 1) * ent_rows], (ent_rows, 128)
                        )
                        line = jnp.transpose(column)[0:8, :]
                        count_ref[step, low] = jnp.broadcast_to(
                            line, (grid[R_HI], 2, 8, ent_rows)
                        )
            agg = jnp.dot(hot_ref[rows, :], message_ref[:, cols], preferred_element_type=f32)
            agg = agg.reshape(2, grid[R_HI], 2, share, half)
            part_ref[step, :, :, :, :, cols] = agg
            part_sent[step, :, :, :, :, cols] = agg.astype(bf16)
            return carry

        lax.fori_loop(0, grid[E_HI], gather_sums, 0)
        if number == 0:
            pl.semaphore_wait(pltpu.get_barrier_semaphore(), greeted)
            counts.start()
        sums[number].start()

    for stage in range(4):
        counts.advance()
        sums[0].advance()
        sums[1].advance()
        if stage < 2:
            for step in range(2 * stage, 2 * stage + 2):
                rows = pl.ds(step * block, block)
                facts_t[:, rows] = jnp.transpose(facts_ref[rows, :])

    lane = lax.broadcasted_iota(jnp.int32, (share, ent_rows), 1)
    row = lax.broadcasted_iota(jnp.int32, (share, ent_rows), 0) + rep * share
    spread_counts = jnp.broadcast_to(counts.own[0:1, :], (share, ent_rows))
    count = jnp.sum(jnp.where(lane == row, spread_counts, 0.0), axis=1, keepdims=True)
    denom = jnp.maximum(count, 1.0)
    agg = jnp.concatenate([sums[0].own[...], sums[1].own[...]], axis=1)
    mean = (agg / denom).astype(bf16)
    zval = jnp.dot(mean, w_upd_ref[...], preferred_element_type=f32)
    grad_z = (cot_ref[rep].astype(f32) * silu_grad(zval)).astype(bf16)
    d_mean = lax.dot_general(
        grad_z, w_upd_ref[...], (((1,), (1,)), ((), ())), preferred_element_type=f32
    )
    all_ref[here] = (d_mean / denom).astype(bf16)
    for item in spreads:
        item.start()
    side = lax.dot_general(grad_z, mean, (((0,), (0,)), ((), ())), preferred_element_type=f32)
    side_ref[...] = side.reshape(side_ref.shape)
    side_sent[...] = side.astype(bf16).reshape(side_ref.shape)
    sides.start()
    ent_ref[rep] = (feats_ref[rep].astype(f32) + zval * jax.nn.sigmoid(zval)).astype(bf16)
    ent_copies = []
    for step in range(1, n_rep):
        copy = pltpu.make_async_remote_copy(
            src_ref=ent_ref.at[rep],
            dst_ref=ent_ref.at[rep],
            send_sem=ent_send.at[step - 1],
            recv_sem=ent_recv.at[step - 1],
            device_id={"rep": lax.rem(rep + step, n_rep)},
            device_id_type=MESH,
        )
        copy.start()
        ent_copies.append(copy)
    for stage in range(4):
        for item in spreads:
            item.advance()
    sides.advance()

    n_ents = ent_rows * grid[E_HI] * grid[E_LO]
    for number in range(2):

        def expand(step, carry):
            rows = pl.ds(pl.multiple_of(step * block, block), block)
            keys = jnp.concatenate([
                jnp.transpose(jnp.broadcast_to(
                    key_ref[:, pl.ds(pl.multiple_of(step * block + at, 128), 128)], (128, 128)
                ))
                for at in range(0, block, 128)
            ], axis=0)
            hits = jnp.concatenate([
                (keys == lax.broadcasted_iota(jnp.int32, (block, 128), 1) + at)
                .astype(f32).astype(bf16)
                for at in range(0, n_ents, 128)
            ], axis=1)
            d_msg = jnp.dot(
                hits, all_ref[...].reshape(n_ents, width), preferred_element_type=f32
            )
            d_pre_ref[rows, :] = (d_msg * gate_ref[rows, :]).astype(bf16)
            return carry

        lax.fori_loop(2 * number, 2 * number + 2, expand, 0)
        sides.advance()
    for number, cols in enumerate(halves):
        left = jnp.dot(facts_t[...], d_pre_ref[:, cols], preferred_element_type=f32)
        left = left.reshape(left_ref.shape[:-1] + (half,))
        left_ref[every + (cols,)] = left
        left_sent[every + (cols,)] = left.astype(bf16)
        lefts[number].start()
        if number == 0:
            sides.advance()
    for stage in range(4):
        for item in lefts:
            item.advance()
    for copy in ent_copies:
        copy.wait()
    grads_ref[:, 0:half] = lefts[0].own[...]
    grads_ref[:, half:width] = lefts[1].own[...]
    grads_ref[:, width:2 * width] = sides.own[...]


def in_vmem(number):
    return [pl.BlockSpec(memory_space=pltpu.VMEM)] * number


def per_device(facts, fact_owner, fact_slot, entity_feats, out_cotangent, w_msg, w_upd):
    n_owners = lax.axis_size("ent")
    n_copies = lax.axis_size("rep")
    grid = (n_owners // 2, 2, n_copies // 2, 2)
    fact_rows, width = facts.shape
    ent_rows = entity_feats.shape[0]
    ents = ent_rows * n_owners
    share = ent_rows // n_copies
    bf16, f32 = jnp.bfloat16, jnp.float32
    rows = width // (n_owners * n_copies)
    half = width // 2
    key = (fact_owner[:, 0] * ent_rows + fact_slot).reshape(1, fact_rows)
    hot_rows = ents if ents <= 1024 else 2 * ent_rows
    rep_sem = pltpu.SemaphoreType.DMA((n_copies - 1,))
    d_pre, ent_out, grads = pl.pallas_call(
        functools.partial(layer_kernel, grid),
        out_shape=(
            jax.ShapeDtypeStruct((fact_rows, width), bf16),
            jax.ShapeDtypeStruct((n_copies, share, width), bf16),
            jax.ShapeDtypeStruct((rows, 2 * width), f32),
        ),
        in_specs=in_vmem(6),
        out_specs=in_vmem(3),
        scratch_shapes=(
            [
                pltpu.VMEM((fact_rows, width), f32),
                pltpu.VMEM(grid + (share, width), f32),
                pltpu.VMEM(grid + (share, width), bf16),
                pltpu.VMEM((hot_rows, fact_rows), bf16),
                pltpu.VMEM((width, fact_rows), bf16),
                pltpu.VMEM(grid + (share, width), bf16),
                pltpu.VMEM(grid + (8, ent_rows), f32),
            ]
            + [
                pltpu.VMEM(grid + (rows, width), f32),
                pltpu.VMEM(grid + (rows, width), bf16),
            ] * 2
            + sum_scratch(grid, ORDER_A, (8, ent_rows), f32)
            + sum_scratch(grid, ORDER_A, (share, half), bf16)
            + sum_scratch(grid, ORDER_B, (share, half), bf16)
            + gather_scratch(grid, ORDER_A[::-1])
            + gather_scratch(grid, ORDER_B[::-1])
            + sum_scratch(grid, ORDER_A, (rows, width), bf16)
            + sum_scratch(grid, ORDER_A, (rows, half), bf16)
            + sum_scratch(grid, ORDER_B, (rows, half), bf16)
            + [rep_sem, rep_sem]
        ),
        compiler_params=pltpu.CompilerParams(
            collective_id=0, has_side_effects=True, vmem_limit_bytes=VMEM_LIMIT
        ),
    )(
        facts,
        key,
        entity_feats.reshape(n_copies, share, width),
        out_cotangent.reshape(n_copies, share, width),
        w_msg,
        w_upd,
    )
    fact_grad = lax.dot_general(
        d_pre, w_msg, (((1,), (1,)), ((), ())), preferred_element_type=f32
    ).astype(bf16)
    return (ent_out.reshape(ent_rows, width), fact_grad, grads[:, :width], grads[:, width:])


def solution(mesh):
    placed = (
        P(("ent", "rep"), None),
        P(("ent", "rep"), None),
        P(("ent", "rep")),
        P("ent", None),
        P("ent", None),
        P(),
        P(),
    )
    return jax.shard_map(
        per_device,
        mesh=mesh,
        in_specs=placed,
        out_specs=(
            P("ent", None),
            P(("ent", "rep"), None),
            P(("ent", "rep"), None),
            P(("ent", "rep"), None),
        ),
        check_vma=False,
    )
```

```python
import functools

import jax
import jax.numpy as jnp
from jax import lax
from jax.experimental import pallas as pl
from jax.experimental.pallas import tpu as pltpu
from jax.sharding import PartitionSpec as P

E_HI, E_LO, R_HI, R_LO = range(4)
ORDER_A = (R_LO, R_HI, E_LO, E_HI)
ORDER_B = (R_LO, E_LO, R_HI, E_HI)
MESH = pl.DeviceIdType.MESH
VMEM_LIMIT = 60 << 20


def silu_grad(value):
    sig = jax.nn.sigmoid(value)
    return sig * (1.0 + value * (1.0 - sig))


def position():
    ent, rep = lax.axis_index("ent"), lax.axis_index("rep")
    return (ent // 2, lax.rem(ent, 2), rep // 2, lax.rem(rep, 2))


def device_at(here, dim, coord):
    if dim == E_HI:
        return {"ent": coord * 2 + here[E_LO]}
    if dim == E_LO:
        return {"ent": here[E_HI] * 2 + coord}
    if dim == R_HI:
        return {"rep": coord * 2 + here[R_LO]}
    return {"rep": here[R_HI] * 2 + coord}


def greet(grid, here):
    barrier = pltpu.get_barrier_semaphore()
    rep = here[R_HI] * 2 + here[R_LO]
    n_rep = grid[R_HI] * grid[R_LO]
    total = 0
    for step in range(1, n_rep):
        pl.semaphore_signal(
            barrier, inc=1, device_id={"rep": lax.rem(rep + step, n_rep)}, device_id_type=MESH
        )
        total += 1
    for dim in (E_HI, E_LO):
        for step in range(1, grid[dim]):
            target = device_at(here, dim, lax.rem(here[dim] + step, grid[dim]))
            pl.semaphore_signal(barrier, inc=1, device_id=target, device_id_type=MESH)
            total += 1
    return total


def sum_scratch(grid, order, tail, dtype):
    left, shapes = [0, 1, 2, 3], []
    for dim in order:
        left.remove(dim)
        kept = tuple(grid[d] for d in left) + tail
        shapes += [
            pltpu.VMEM((grid[dim] - 1,) + kept, dtype),
            pltpu.VMEM(kept, jnp.float32),
            pltpu.VMEM(kept if left else (16, 128), dtype),
            pltpu.SemaphoreType.DMA((grid[dim] - 1,)),
            pltpu.SemaphoreType.DMA((grid[dim] - 1,)),
        ]
    return shapes


class Scatter:
    def __init__(self, grid, here, order, own, sent, scratch):
        self.grid, self.here, self.order, self.own, self.sent = grid, here, order, own, sent
        self.scratch, self.left, self.stage = scratch, [0, 1, 2, 3], 0

    def start(self):
        dim = self.order[self.stage]
        size, mine = self.grid[dim], self.here[dim]
        arrived, _, _, send, recv = self.scratch[5 * self.stage:5 * self.stage + 5]
        lead = (slice(None),) * self.left.index(dim)
        self.copies = []
        for step in range(1, size):
            coord = lax.rem(mine + step, size)
            copy = pltpu.make_async_remote_copy(
                src_ref=self.sent.at[lead + (coord,)],
                dst_ref=arrived.at[step - 1],
                send_sem=send.at[step - 1],
                recv_sem=recv.at[step - 1],
                device_id=device_at(self.here, dim, coord),
                device_id_type=MESH,
            )
            copy.start()
            self.copies.append(copy)

    def finish(self):
        dim = self.order[self.stage]
        arrived, total, rounded, _, _ = self.scratch[5 * self.stage:5 * self.stage + 5]
        lead = (slice(None),) * self.left.index(dim)
        value = self.own[lead + (self.here[dim],)]
        for index, copy in enumerate(self.copies):
            copy.wait()
            value = value + arrived[index].astype(jnp.float32)
        total[...] = value
        self.own = self.sent = total
        self.left.remove(dim)
        self.stage += 1
        if self.left and rounded.dtype != jnp.float32:
            rounded[...] = value.astype(rounded.dtype)
            self.sent = rounded

    def advance(self):
        self.finish()
        if self.stage < 4:
            self.start()


class Gather:
    def __init__(self, grid, here, order, columns, ref, sems):
        self.grid, self.here, self.order = grid, here, order
        self.columns, self.ref, self.sems = columns, ref, sems
        self.done, self.stage = [], 0

    def start(self):
        dim = self.order[self.stage]
        size, mine = self.grid[dim], self.here[dim]
        send, recv = self.sems[2 * self.stage:2 * self.stage + 2]
        index = tuple(slice(None) if d in self.done else self.here[d] for d in range(4))
        block = self.ref.at[index + (slice(None), self.columns)]
        self.copies = []
        for step in range(1, size):
            coord = lax.rem(mine + step, size)
            copy = pltpu.make_async_remote_copy(
                src_ref=block,
                dst_ref=block,
                send_sem=send.at[step - 1],
                recv_sem=recv.at[step - 1],
                device_id=device_at(self.here, dim, coord),
                device_id_type=MESH,
            )
            copy.start()
            self.copies.append(copy)

    def advance(self):
        for copy in self.copies:
            copy.wait()
        self.done.append(self.order[self.stage])
        self.stage += 1
        if self.stage < 4:
            self.start()


def gather_scratch(grid, order):
    return [pltpu.SemaphoreType.DMA((grid[d] - 1,)) for d in order for _ in range(2)]


def layer_kernel(grid, facts_ref, owner_ref, slot_ref, feats_ref, cot_ref, w_ref, w_upd_ref,
                 fact_ref, ent_ref, msg_ref, upd_ref, *scratch):
    bf16, f32 = jnp.bfloat16, jnp.float32
    here = position()
    rep = lax.axis_index("rep")
    n_rep = grid[R_HI] * grid[R_LO]
    greeted = greet(grid, here)
    scratch = list(scratch)

    def take(number):
        taken, scratch[:number] = scratch[:number], []
        return taken

    gate_ref, part_ref, part_sent, hot_ref, facts_t, all_ref, count_ref = take(7)
    side_ref, side_sent, left_ref, left_sent = take(4)
    d_pre_ref, key_ref, hits_ref = take(3)
    message_ref = d_pre_ref
    fact_rows, width = facts_ref.shape
    half = width // 2
    halves = [slice(0, half), slice(half, width)]
    share = part_ref.shape[-2]
    ent_rows = share * n_rep
    block = fact_rows // 4
    pair = 2 * ent_rows
    kept = hot_ref.shape[0] > pair
    n_ents = ent_rows * grid[E_HI] * grid[E_LO]
    key_ref[...] = owner_ref[...] * ent_rows + slot_ref[...]
    every = (slice(None),) * 5
    counts = Scatter(grid, here, ORDER_A, count_ref, count_ref, take(20))
    sums = [
        Scatter(grid, here, order, part_ref.at[every + (cols,)], part_sent.at[every + (cols,)],
                take(20))
        for order, cols in zip((ORDER_A, ORDER_B), halves)
    ]
    spreads = [
        Gather(grid, here, order[::-1], cols, all_ref, take(8))
        for order, cols in zip((ORDER_A, ORDER_B), halves)
    ]
    sides = Scatter(grid, here, ORDER_A, side_ref, side_sent, take(20))
    lefts = [
        Scatter(grid, here, order, left_ref.at[every + (cols,)], left_sent.at[every + (cols,)],
                take(20))
        for order, cols in zip((ORDER_A, ORDER_B), halves)
    ]
    ent_send, ent_recv = take(2)

    for number, cols in enumerate(halves):

        def project(step, carry, cols=cols):
            rows = pl.ds(pl.multiple_of(step * block, block), block)
            pre = jnp.dot(facts_ref[rows, :], w_ref[:, cols], preferred_element_type=f32)
            sig = jax.nn.sigmoid(pre)
            gate_ref[rows, cols] = sig * (1.0 + pre * (1.0 - sig))
            message_ref[rows, cols] = (pre * sig).astype(bf16)
            return carry

        lax.fori_loop(0, 4, project, 0)

        def gather_sums(step, carry, number=number, cols=cols):
            rows = pl.ds(pl.multiple_of(step * pair, pair), pair) if kept else pl.ds(0, pair)
            if number == 0 or not kept:
                ids = lax.broadcasted_iota(jnp.int32, (pair, fact_rows), 0) + step * pair
                hit = (ids == key_ref[...]).astype(f32)
                hot_ref[rows, :] = hit.astype(bf16)
                if number == 0:
                    total = jnp.sum(hit, axis=1, keepdims=True)
                    for low in range(2):
                        column = jnp.broadcast_to(
                            total[low * ent_rows:(low + 1) * ent_rows], (ent_rows, 128)
                        )
                        line = jnp.transpose(column)[0:8, :]
                        count_ref[step, low] = jnp.broadcast_to(
                            line, (grid[R_HI], 2, 8, ent_rows)
                        )
            agg = jnp.dot(hot_ref[rows, :], message_ref[:, cols], preferred_element_type=f32)
            agg = agg.reshape(2, grid[R_HI], 2, share, half)
            part_ref[step, :, :, :, :, cols] = agg
            part_sent[step, :, :, :, :, cols] = agg.astype(bf16)
            return carry

        lax.fori_loop(0, grid[E_HI], gather_sums, 0)
        if number == 0:
            pl.semaphore_wait(pltpu.get_barrier_semaphore(), greeted)
            counts.start()
        sums[number].start()

    for stage in range(4):
        counts.advance()
        sums[0].advance()
        sums[1].advance()
        if stage < 2:
            for step in range(2 * stage, 2 * stage + 2):
                rows = pl.ds(step * block, block)
                facts_t[:, rows] = jnp.transpose(facts_ref[rows, :])

    lane = lax.broadcasted_iota(jnp.int32, (share, ent_rows), 1)
    row = lax.broadcasted_iota(jnp.int32, (share, ent_rows), 0) + rep * share
    spread_counts = jnp.broadcast_to(counts.own[0:1, :], (share, ent_rows))
    count = jnp.sum(jnp.where(lane == row, spread_counts, 0.0), axis=1, keepdims=True)
    denom = jnp.maximum(count, 1.0)
    agg = jnp.concatenate([sums[0].own[...], sums[1].own[...]], axis=1)
    mean = (agg / denom).astype(bf16)
    zval = jnp.dot(mean, w_upd_ref[...], preferred_element_type=f32)
    grad_z = (cot_ref[rep].astype(f32) * silu_grad(zval)).astype(bf16)
    d_mean = lax.dot_general(
        grad_z, w_upd_ref[...], (((1,), (1,)), ((), ())), preferred_element_type=f32
    )
    all_ref[here] = (d_mean / denom).astype(bf16)
    for item in spreads:
        item.start()
    side = lax.dot_general(grad_z, mean, (((0,), (0,)), ((), ())), preferred_element_type=f32)
    side_ref[...] = side.reshape(side_ref.shape)
    side_sent[...] = side.astype(bf16).reshape(side_ref.shape)
    sides.start()
    ent_ref[rep] = (feats_ref[rep].astype(f32) + zval * jax.nn.sigmoid(zval)).astype(bf16)
    ent_copies = []
    for step in range(1, n_rep):
        copy = pltpu.make_async_remote_copy(
            src_ref=ent_ref.at[rep],
            dst_ref=ent_ref.at[rep],
            send_sem=ent_send.at[step - 1],
            recv_sem=ent_recv.at[step - 1],
            device_id={"rep": lax.rem(rep + step, n_rep)},
            device_id_type=MESH,
        )
        copy.start()
        ent_copies.append(copy)

    piece = block if kept else block // 4
    pieces = fact_rows // piece

    def build_hits(step):
        keys = jnp.concatenate([
            jnp.transpose(jnp.broadcast_to(
                key_ref[:, pl.ds(pl.multiple_of(step * piece + at, 128), 128)], (128, 128)
            ))
            for at in range(0, piece, 128)
        ], axis=0)
        place = pl.ds(pl.multiple_of(step * piece, piece), piece) if kept else pl.ds(0, piece)
        for at in range(0, n_ents, 128):
            ids = lax.broadcasted_iota(jnp.int32, (piece, 128), 1) + at
            hits_ref[place, at:at + 128] = (keys == ids).astype(f32).astype(bf16)

    for stage in range(4):
        if kept:
            build_hits(stage)
        for item in spreads:
            item.advance()
    sides.advance()

    for number in range(2):

        def expand(step, carry):
            rows = pl.ds(pl.multiple_of(step * piece, piece), piece)
            if not kept:
                build_hits(step)
            hits = hits_ref[rows if kept else pl.ds(0, piece), :]
            d_msg = jnp.dot(
                hits, all_ref[...].reshape(n_ents, width), preferred_element_type=f32
            )
            d_pre_ref[rows, :] = (d_msg * gate_ref[rows, :]).astype(bf16)
            return carry

        lax.fori_loop(number * pieces // 2, (number + 1) * pieces // 2, expand, 0)
        sides.advance()
    for number, cols in enumerate(halves):
        left = jnp.dot(facts_t[...], d_pre_ref[:, cols], preferred_element_type=f32)
        left = left.reshape(left_ref.shape[:-1] + (half,))
        left_ref[every + (cols,)] = left
        left_sent[every + (cols,)] = left.astype(bf16)
        lefts[number].start()
        if number == 0:
            sides.advance()
    for stage in range(4):
        rows = pl.ds(stage * block, block)
        fact_ref[rows, :] = lax.dot_general(
            d_pre_ref[rows, :], w_ref[...], (((1,), (1,)), ((), ())), preferred_element_type=f32
        ).astype(bf16)
        for item in lefts:
            item.advance()
    for copy in ent_copies:
        copy.wait()
    msg_ref[:, 0:half] = lefts[0].own[...]
    msg_ref[:, half:width] = lefts[1].own[...]
    upd_ref[...] = sides.own[...]


def hand_over_kernel(*refs):
    number = (len(refs) - 1) // 2
    sems = refs[-1]
    copies = []
    for index in range(number):
        source, target = refs[index], refs[number + index]
        parts = 4 if index == 0 else 1
        rows = source.shape[0] // parts
        for part in range(parts):
            place = pl.ds(part * rows, rows)
            copy = pltpu.make_async_copy(
                source.at[place], target.at[place], sems.at[len(copies)]
            )
            copy.start()
            copies.append(copy)
    for copy in copies:
        copy.wait()


def in_vmem(number):
    return [pl.BlockSpec(memory_space=pltpu.VMEM)] * number


def per_device(facts, fact_owner, fact_slot, entity_feats, out_cotangent, w_msg, w_upd):
    n_owners = lax.axis_size("ent")
    n_copies = lax.axis_size("rep")
    grid = (n_owners // 2, 2, n_copies // 2, 2)
    fact_rows, width = facts.shape
    ent_rows = entity_feats.shape[0]
    ents = ent_rows * n_owners
    share = ent_rows // n_copies
    bf16, f32 = jnp.bfloat16, jnp.float32
    rows = width // (n_owners * n_copies)
    half = width // 2
    hot_rows = ents if ents <= 1024 else 2 * ent_rows
    rep_sem = pltpu.SemaphoreType.DMA((n_copies - 1,))
    results = pl.pallas_call(
        functools.partial(layer_kernel, grid),
        out_shape=(
            jax.ShapeDtypeStruct((fact_rows, width), bf16),
            jax.ShapeDtypeStruct((n_copies, share, width), bf16),
            jax.ShapeDtypeStruct((rows, width), f32),
            jax.ShapeDtypeStruct((rows, width), f32),
        ),
        in_specs=in_vmem(7),
        out_specs=in_vmem(4),
        scratch_shapes=(
            [
                pltpu.VMEM((fact_rows, width), f32),
                pltpu.VMEM(grid + (share, width), f32),
                pltpu.VMEM(grid + (share, width), bf16),
                pltpu.VMEM((hot_rows, fact_rows), bf16),
                pltpu.VMEM((width, fact_rows), bf16),
                pltpu.VMEM(grid + (share, width), bf16),
                pltpu.VMEM(grid + (8, ent_rows), f32),
            ]
            + [
                pltpu.VMEM(grid + (rows, width), f32),
                pltpu.VMEM(grid + (rows, width), bf16),
            ] * 2
            + [
                pltpu.VMEM((fact_rows, width), bf16),
                pltpu.VMEM((1, fact_rows), jnp.int32),
                pltpu.VMEM((fact_rows if ents <= 1024 else fact_rows // 16, ents), bf16),
            ]
            + sum_scratch(grid, ORDER_A, (8, ent_rows), f32)
            + sum_scratch(grid, ORDER_A, (share, half), bf16)
            + sum_scratch(grid, ORDER_B, (share, half), bf16)
            + gather_scratch(grid, ORDER_A[::-1])
            + gather_scratch(grid, ORDER_B[::-1])
            + sum_scratch(grid, ORDER_A, (rows, width), bf16)
            + sum_scratch(grid, ORDER_A, (rows, half), bf16)
            + sum_scratch(grid, ORDER_B, (rows, half), bf16)
            + [rep_sem, rep_sem]
        ),
        compiler_params=pltpu.CompilerParams(
            collective_id=0, has_side_effects=True, vmem_limit_bytes=VMEM_LIMIT
        ),
    )(
        facts,
        fact_owner.reshape(1, fact_rows),
        fact_slot.reshape(1, fact_rows),
        entity_feats.reshape(n_copies, share, width),
        out_cotangent.reshape(n_copies, share, width),
        w_msg,
        w_upd,
    )
    fact_grad, ent_out, msg_grad, upd_grad = pl.pallas_call(
        hand_over_kernel,
        out_shape=tuple(jax.ShapeDtypeStruct(item.shape, item.dtype) for item in results),
        in_specs=[pl.BlockSpec(memory_space=pl.ANY)] * 4,
        out_specs=tuple([pl.BlockSpec(memory_space=pl.ANY)] * 4),
        scratch_shapes=[pltpu.SemaphoreType.DMA((7,))],
    )(*results)
    return (ent_out.reshape(ent_rows, width), fact_grad, msg_grad, upd_grad)


def solution(mesh):
    placed = (
        P(("ent", "rep"), None),
        P(("ent", "rep"), None),
        P(("ent", "rep")),
        P("ent", None),
        P("ent", None),
        P(),
        P(),
    )
    return jax.shard_map(
        per_device,
        mesh=mesh,
        in_specs=placed,
        out_specs=(
            P("ent", None),
            P(("ent", "rep"), None),
            P(("ent", "rep"), None),
            P(("ent", "rep"), None),
        ),
        check_vma=False,
    )
```
